32 devices in a mesh: parts: 2 (over x), sta: 16 (over z, y, core).
Axes of the slice: x: 2, y: 2, z: 4, core: 2. Of those that a mesh axis runs over, the one named last changes fastest.
Arguments:
- records: bfloat16 [32, 3, 2478], P('sta', None, 'parts'), parts along dimension 2, may hold values from -6 to 6
- templates: bfloat16 [32, 32, 3, 600], P(None, 'sta'), may hold values from -6 to 6
- shifts: int32 [32, 32], replicated, may hold values from 0 to 512, as said below
- present: int32 [32], replicated, may hold values 0 or 1
Outputs:
- detection: float32 [32, 256], P('sta', 'parts'), parts along dimension 1
The draws below stay inside these ranges and needn't reach their ends.
There are 2 independent parts, one for each index of `parts`. The reference program is written for one: setup_inputs(seed, part) draws one part's arguments, and reference() takes and returns one part's arrays. A program takes and returns all parts, laid end to end along the dimension named above; an argument that names none is the same for every part. Nothing has to cross between parts.
Inputs may be any that keep to these rules, and one draw needn't show every extreme that they name: `shifts`: for every template some station has moveout exactly 512 and some station moveout 0.
All inputs are finite; a program needn't handle non-finite values.
Results may differ from the reference program's by a relative error of at most 0.0029.
Values may be sent and summed in bfloat16 or wider, within the bound.
A program may use at most 64 MiB of HBM per device.

```python
import math
import jax
import jax.numpy as jnp
from jax import lax

LEN = 600
WIN = 640
MAXSHIFT = 512
STATIONS = 32
TEMPL = 32
SAMPLES = 1239


def draw_shifts(key, part):
    first = jax.random.fold_in(key, 11)
    second = jax.random.fold_in(key, 12)
    third = jax.random.fold_in(key, 13)
    base = jax.random.randint(first, (TEMPL, STATIONS), 0, MAXSHIFT + 1, dtype=jnp.int32)
    upper = jax.random.randint(second, (TEMPL,), 0, STATIONS, dtype=jnp.int32)
    lower = (upper + jax.random.randint(third, (TEMPL,), 1, STATIONS, dtype=jnp.int32)) % STATIONS
    column = jnp.arange(STATIONS, dtype=jnp.int32)[None, :]
    base = jnp.where(column == upper[:, None], MAXSHIFT, base)
    base = jnp.where(column == lower[:, None], 0, base)
    return base.astype(jnp.int32)


def plant(array, key, least, high):
    index_at = [jax.random.randint(jax.random.fold_in(key, axis), (), 0, length) for axis, length in enumerate(array.shape)]
    widest = array.shape.index(max(array.shape))
    beside = index_at[:widest] + [(index_at[widest] + 1) % array.shape[widest]] + index_at[widest + 1:]
    return array.at[tuple(index_at)].set(least).at[tuple(beside)].set(high)


def levels(key, shape, split, least, largest):
    def one(position, blocks):
        heights = jax.random.uniform(jax.random.fold_in(jax.random.fold_in(key, 6), position), (blocks,), jnp.float32, least / len(split), largest / len(split))
        return jnp.repeat(jnp.exp(heights), shape[position] // blocks).reshape((-1,) + (1,) * (len(shape) - position - 1))

    gain = one(*split[0])
    for cut in split[1:]:
        gain = gain * one(*cut)
    return gain


def gaussian(key, shape, spread, bound, shards=(), held_as=jnp.bfloat16):
    values = spread * jax.random.normal(key, shape, jnp.float32)
    if shards:
        values = values * levels(key, shape, shards, -0.22, 0.18)
    return jnp.clip(values, -bound, bound).astype(held_as)


def setup_inputs(seed: int = 0, part: int = 0) -> dict:
    keys = jax.random.split(jax.random.key(seed), 5)
    part_splits = jax.random.split(jax.random.fold_in(keys[4], part), 5)
    return {
        "records": gaussian(part_splits[0], (STATIONS, 3, SAMPLES), 1.0, 6.0, ((0, 16),)),
        "templates": gaussian(keys[1], (TEMPL, STATIONS, 3, LEN), 1.0, 6.0, ((1, 16),)),
        "shifts": draw_shifts(jax.random.fold_in(keys[4], 71), part),
        "present": plant((jax.random.randint(keys[3], (STATIONS,), 0, 4) < 3).astype(jnp.int32), jax.random.fold_in(keys[3], 1), 0, 1),
    }


def shift_rows(ncc, lags, count_out):

    def pick(row, lag):
        return lax.dynamic_slice_in_dim(row, lag.astype(jnp.int32), count_out, 0)
    return jax.vmap(pick)(ncc, lags)

def station_term(chosen, trace, lags, flag):
    values = chosen.astype(jnp.float32)
    power = lax.optimization_barrier(jnp.mean(values * values, axis=(1, 2), keepdims=True))
    normed = (values * lax.rsqrt(power + 1e-06)).astype(jnp.bfloat16)
    raw = lax.conv_general_dilated(trace[None], normed, (1,), 'VALID', dimension_numbers=('NCH', 'OIH', 'NCH'), preferred_element_type=jnp.float32)[0]
    energy = lax.optimization_barrier(jnp.sum(jnp.square(trace.astype(jnp.float32)), axis=0))
    running = jnp.concatenate([jnp.zeros((1,), jnp.float32), jnp.cumsum(energy)])
    window = (running[LEN:] - running[:-LEN]) / (3 * LEN)
    width = raw.shape[1]
    ncc = raw * lax.rsqrt(window + 1e-06)[None, :] / (3 * LEN)
    moved = shift_rows(ncc, lags, width - MAXSHIFT)
    return moved * flag.astype(jnp.float32)

def reference(records, templates, shifts, present):
    total = jnp.zeros((TEMPL, WIN - MAXSHIFT), jnp.float32)

    def visit(station, carry):
        chosen = lax.dynamic_index_in_dim(templates, station, 1, keepdims=False)
        trace = lax.dynamic_index_in_dim(records, station, 0, keepdims=False)
        lags = lax.dynamic_index_in_dim(shifts, station, 1, keepdims=False)
        flag = lax.dynamic_index_in_dim(present, station, 0, keepdims=False)
        return carry + station_term(chosen, trace, lags, flag)
    total = lax.fori_loop(0, STATIONS, visit, total)
    return total * math.sqrt(3 * LEN / STATIONS)
```

```python
import functools
import math

import jax
import jax.numpy as jnp
from jax import lax
from jax.experimental import pallas as pl
from jax.experimental.pallas import tpu as pltpu
from jax.sharding import PartitionSpec as P

LEN = 600
WIN = 640
MAXSHIFT = 512
OUT = WIN - MAXSHIFT
LANES = 128
TAPS = -(-LEN // LANES)
WIDE = WIN + TAPS * LANES


def window_sums(energy):
    powers = {1: energy}
    size = 1
    while size * 2 <= LEN:
        powers[size * 2] = powers[size] + pltpu.roll(powers[size], size, 1)
        size *= 2
    total, done = None, 0
    while size:
        if LEN & size:
            term = powers[size] if done == 0 else pltpu.roll(powers[size], done, 1)
            total = term if total is None else total + term
            done += size
        size //= 2
    return total


def mirrored(x):
    flip = LANES - 1 - lax.broadcasted_iota(jnp.int32, (x.shape[0], LANES), 1)
    tiles = [
        jnp.take_along_axis(x[:, i : i + LANES], flip, axis=1) for i in range(0, x.shape[1], LANES)
    ]
    return jnp.concatenate(tiles[::-1], axis=1)


def kernel(
    n, rec_hbm, tem_hbm, shift_hbm, present_hbm, out_ref,
    rec_in, tem_in, shift_v, present_s, rec, tem, hank, total, recv,
    in_sem, send_sem, recv_sem,
):
    me = lax.axis_index("sta")
    templ, local = tem_in.shape[0], tem_in.shape[2]
    rows = templ // n
    pitch = tem.shape[1] // templ
    samples = rec_in.shape[2]
    stations = n * local

    loads = [
        pltpu.make_async_copy(src, dst, in_sem.at[i])
        for i, (src, dst) in enumerate(
            [(rec_hbm, rec_in), (tem_hbm, tem_in), (shift_hbm, shift_v), (present_hbm, present_s)]
        )
    ]
    for load in loads:
        load.start()

    barrier = pltpu.get_barrier_semaphore()
    for step in range(1, n):
        pl.semaphore_signal(
            barrier, inc=1, device_id={"sta": lax.rem(me + step, n)},
            device_id_type=pl.DeviceIdType.MESH,
        )

    rec[...] = jnp.zeros_like(rec)
    tem[TAPS - 1] = jnp.zeros((templ * pitch, LANES), jnp.float32)

    loads[0].wait()
    for s in range(local):
        rec[s, 0:3, 0:samples] = rec_in[:, s].astype(jnp.float32)
    turned = [mirrored(rec[s]) for s in range(local)]
    energy = [jnp.sum(x * x, axis=0, keepdims=True) for x in turned]
    window = window_sums(jnp.concatenate(energy, axis=0))[:, WIDE - WIN :] / (3 * LEN)
    inv = lax.rsqrt(window + 1e-06)

    for s in range(local):
        for c in range(3):
            row = jnp.broadcast_to(turned[s][c : c + 1, :], (LANES, WIDE))
            slid = pltpu.roll(row, 0, 1, stride=1, stride_axis=0)
            hank[s, pl.ds(c * LANES, LANES), :] = slid.astype(jnp.bfloat16)

    loads[1].wait()
    for t in range(templ):
        for c in range(3):
            wave = tem_in[t, c].astype(jnp.float32)
            for a in range(TAPS):
                span = min(LANES, LEN - a * LANES)
                tem[a, pl.ds(pitch * t + local * c, local), 0:span] = wave[:, a * LANES : a * LANES + span]

    loads[2].wait()
    loads[3].wait()
    lags_all = shift_v[...].astype(jnp.float32)
    column = lax.broadcasted_iota(jnp.int32, lags_all.shape, 1)
    lane = lax.broadcasted_iota(jnp.int32, (templ, LANES), 1)
    scale = math.sqrt(3 * LEN / stations) / (3 * LEN)
    acc = jnp.zeros((templ, OUT), jnp.float32)
    for s in range(local):
        station = me * local + s
        square = jnp.zeros((templ, LANES), jnp.float32)
        raw = jnp.zeros((templ, WIN), jnp.float32)
        for a in range(TAPS):
            pieces = [tem[a, pl.ds(local * c + s, templ, stride=pitch), :] for c in range(3)]
            square = square + sum(p * p for p in pieces)
            left = jnp.concatenate(pieces, axis=1)
            raw = raw + jnp.dot(
                left.astype(jnp.bfloat16), hank[s, :, pl.ds(WIDE - WIN - a * LANES, WIN)], preferred_element_type=jnp.float32
            )
        power = jnp.sum(square, axis=1, keepdims=True) / (3 * LEN)
        ncc = raw * inv[s : s + 1, :]
        lag = jnp.sum(jnp.where(column == station, lags_all, 0.0), axis=1, keepdims=True)
        lag = jnp.broadcast_to(lag.astype(jnp.int32), (templ, LANES))
        coarse, fine = lag // LANES, lag % LANES
        tiles = [ncc[:, i * LANES : (i + 1) * LANES] for i in range(WIN // LANES)][::-1]
        near, far = tiles[0], tiles[1]
        for i in range(1, len(tiles)):
            near = jnp.where(coarse == i, tiles[i], near)
            if i + 1 < len(tiles):
                far = jnp.where(coarse == i, tiles[i + 1], far)
        at = lane + fine
        index = LANES - 1 - at % LANES
        picked = jnp.where(
            at < LANES,
            jnp.take_along_axis(near, index, axis=1),
            jnp.take_along_axis(far, index, axis=1),
        )
        flag = present_s[station].astype(jnp.float32)
        acc = acc + picked * (lax.rsqrt(power + 1e-06) * (flag * scale))
    for d in range(n):
        total[d] = acc[d * rows : (d + 1) * rows]

    pl.semaphore_wait(barrier, n - 1)
    for step in range(1, n):
        to = lax.rem(me + step, n)
        pltpu.make_async_remote_copy(
            src_ref=total.at[to], dst_ref=recv.at[step], send_sem=send_sem, recv_sem=recv_sem,
            device_id={"sta": to}, device_id_type=pl.DeviceIdType.MESH,
        ).start()
    rest = recv.at[pl.ds(1, n - 1)]
    pltpu.make_async_copy(rest, rest, recv_sem).wait()
    pltpu.make_async_copy(rest, rest, send_sem).wait()
    out_ref[...] = total[me] + jnp.sum(recv[pl.ds(1, n - 1)], axis=0)


def body(records, templates, shifts, present):
    n = lax.axis_size("sta")
    templ, local = templates.shape[0], templates.shape[1]
    rows = templ // n
    pitch = -(-3 * local // 8) * 8
    records = records.transpose(1, 0, 2)
    templates = templates.transpose(0, 2, 1, 3)
    hbm = pl.BlockSpec(memory_space=pl.ANY)
    return pl.pallas_call(
        functools.partial(kernel, n),
        out_shape=jax.ShapeDtypeStruct((rows, OUT), jnp.float32),
        in_specs=[hbm] * 4,
        out_specs=pl.BlockSpec(memory_space=pltpu.VMEM),
        scratch_shapes=[
            pltpu.VMEM(records.shape, records.dtype),
            pltpu.VMEM(templates.shape, templates.dtype),
            pltpu.VMEM(shifts.shape, shifts.dtype),
            pltpu.SMEM(present.shape, present.dtype),
            pltpu.VMEM((local, 8, WIDE), jnp.float32),
            pltpu.VMEM((TAPS, templ * pitch, LANES), jnp.float32),
            pltpu.VMEM((local, 3 * LANES, WIDE), jnp.bfloat16),
            pltpu.VMEM((n, rows, OUT), jnp.float32),
            pltpu.VMEM((n, rows, OUT), jnp.float32),
            pltpu.SemaphoreType.DMA((4,)),
            pltpu.SemaphoreType.DMA,
            pltpu.SemaphoreType.DMA,
        ],
        compiler_params=pltpu.CompilerParams(collective_id=0, has_side_effects=True),
    )(records, templates, shifts, present)


def solution(mesh):
    placed = (P("sta", None, "parts"), P(None, "sta", None, None), P(), P())
    return jax.shard_map(
        body, mesh=mesh, in_specs=placed, out_specs=P("sta", "parts"), check_vma=False
    )
```

```python
import functools
import math

import jax
import jax.numpy as jnp
from jax import lax
from jax.experimental import pallas as pl
from jax.experimental.pallas import tpu as pltpu
from jax.sharding import PartitionSpec as P

LEN = 600
WIN = 640
MAXSHIFT = 512
OUT = WIN - MAXSHIFT
LANES = 128
TAPS = -(-LEN // LANES)
WIDE = WIN + TAPS * LANES


def window_sums(energy):
    powers = {1: energy}
    size = 1
    while size * 2 <= LEN:
        powers[size * 2] = powers[size] + pltpu.roll(powers[size], size, 1)
        size *= 2
    total, done = None, 0
    while size:
        if LEN & size:
            term = powers[size] if done == 0 else pltpu.roll(powers[size], done, 1)
            total = term if total is None else total + term
            done += size
        size //= 2
    return total


def mirrored(x):
    flip = LANES - 1 - lax.broadcasted_iota(jnp.int32, (x.shape[0], LANES), 1)
    tiles = [
        jnp.take_along_axis(x[:, i : i + LANES], flip, axis=1) for i in range(0, x.shape[1], LANES)
    ]
    return jnp.concatenate(tiles[::-1], axis=1)


def kernel(
    n, rec_hbm, tem_hbm, shift_hbm, present_hbm, out_ref,
    rec_in, tem_in, shift_v, present_s, rec, tem, hank, total, recv,
    in_sem, send_sem, recv_sem,
):
    me = lax.axis_index("sta")
    templ, local = tem_in.shape[0], tem_in.shape[2]
    rows = templ // n
    pitch = tem.shape[1] // templ
    samples = rec_in.shape[2]
    stations = n * local

    loads = [
        pltpu.make_async_copy(src, dst, in_sem.at[i])
        for i, (src, dst) in enumerate(
            [(rec_hbm, rec_in), (tem_hbm, tem_in), (shift_hbm, shift_v), (present_hbm, present_s)]
        )
    ]
    for load in loads:
        load.start()

    barrier = pltpu.get_barrier_semaphore()
    for step in range(1, n):
        pl.semaphore_signal(
            barrier, inc=1, device_id={"sta": lax.rem(me + step, n)},
            device_id_type=pl.DeviceIdType.MESH,
        )

    rec[...] = jnp.zeros_like(rec)
    tem[TAPS - 1] = jnp.zeros((templ * pitch, LANES), jnp.float32)

    loads[0].wait()
    for s in range(local):
        rec[s, 0:3, 0:samples] = rec_in[:, s].astype(jnp.float32)
    turned = [mirrored(rec[s]) for s in range(local)]
    energy = [jnp.sum(x * x, axis=0, keepdims=True) for x in turned]
    window = window_sums(jnp.concatenate(energy, axis=0))[:, WIDE - WIN :] / (3 * LEN)
    inv = lax.rsqrt(window + 1e-06)

    for s in range(local):
        for c in range(3):
            row = jnp.broadcast_to(turned[s][c : c + 1, :], (LANES, WIDE))
            slid = pltpu.roll(row, 0, 1, stride=1, stride_axis=0)
            hank[s, pl.ds(c * LANES, LANES), :] = slid.astype(jnp.bfloat16)

    loads[1].wait()
    for t in range(templ):
        for c in range(3):
            wave = tem_in[t, c].astype(jnp.float32)
            for a in range(TAPS):
                span = min(LANES, LEN - a * LANES)
                tem[a, pl.ds(pitch * t + local * c, local), 0:span] = wave[:, a * LANES : a * LANES + span]

    loads[2].wait()
    loads[3].wait()
    lags_all = shift_v[...].astype(jnp.float32)
    column = lax.broadcasted_iota(jnp.int32, lags_all.shape, 1)
    lane = lax.broadcasted_iota(jnp.int32, (templ, LANES), 1)
    scale = math.sqrt(3 * LEN / stations) / (3 * LEN)
    acc = jnp.zeros((templ, OUT), jnp.float32)
    for s in range(local):
        station = me * local + s
        square = jnp.zeros((templ, LANES), jnp.float32)
        raw = jnp.zeros((templ, WIN), jnp.float32)
        for a in range(TAPS):
            pieces = [tem[a, pl.ds(local * c + s, templ, stride=pitch), :] for c in range(3)]
            square = square + sum(p * p for p in pieces)
            left = jnp.concatenate(pieces, axis=1)
            raw = raw + jnp.dot(
                left.astype(jnp.bfloat16), hank[s, :, pl.ds(WIDE - WIN - a * LANES, WIN)], preferred_element_type=jnp.float32
            )
        power = jnp.sum(square, axis=1, keepdims=True) / (3 * LEN)
        ncc = raw * inv[s : s + 1, :]
        lag = jnp.sum(jnp.where(column == station, lags_all, 0.0), axis=1, keepdims=True)
        lag = jnp.broadcast_to(lag.astype(jnp.int32), (templ, LANES))
        coarse, fine = lag // LANES, lag % LANES
        tiles = [ncc[:, i * LANES : (i + 1) * LANES] for i in range(WIN // LANES)][::-1]
        near, far = tiles[0], tiles[1]
        for i in range(1, len(tiles)):
            near = jnp.where(coarse == i, tiles[i], near)
            if i + 1 < len(tiles):
                far = jnp.where(coarse == i, tiles[i + 1], far)
        at = lane + fine
        index = LANES - 1 - at % LANES
        picked = jnp.where(
            at < LANES,
            jnp.take_along_axis(near, index, axis=1),
            jnp.take_along_axis(far, index, axis=1),
        )
        flag = present_s[station].astype(jnp.float32)
        acc = acc + picked * (lax.rsqrt(power + 1e-06) * (flag * scale))
    for d in range(n):
        total[d] = acc[d * rows : (d + 1) * rows]

    pl.semaphore_wait(barrier, n - 1)
    for step in range(1, n):
        to = lax.rem(me + step, n)
        pltpu.make_async_remote_copy(
            src_ref=total.at[to], dst_ref=recv.at[step], send_sem=send_sem, recv_sem=recv_sem,
            device_id={"sta": to}, device_id_type=pl.DeviceIdType.MESH,
        ).start()
    rest = recv.at[pl.ds(1, n - 1)]
    pltpu.make_async_copy(rest, rest, recv_sem).wait()
    pltpu.make_async_copy(rest, rest, send_sem).wait()
    out_ref[...] = total[me] + jnp.sum(recv[pl.ds(1, n - 1)], axis=0)


def body(records, templates, shifts, present):
    n = lax.axis_size("sta")
    templ, local = templates.shape[0], templates.shape[1]
    rows = templ // n
    pitch = -(-3 * local // 8) * 8
    records = records.transpose(1, 0, 2)
    templates = templates.transpose(0, 2, 1, 3)
    hbm = pl.BlockSpec(memory_space=pl.ANY)
    return pl.pallas_call(
        functools.partial(kernel, n),
        out_shape=jax.ShapeDtypeStruct((rows, OUT), jnp.float32),
        in_specs=[hbm] * 4,
        out_specs=pl.BlockSpec(memory_space=pltpu.VMEM),
        scratch_shapes=[
            pltpu.VMEM(records.shape, records.dtype),
            pltpu.VMEM(templates.shape, templates.dtype),
            pltpu.VMEM(shifts.shape, shifts.dtype),
            pltpu.SMEM(present.shape, present.dtype),
            pltpu.VMEM((local, 8, WIDE), jnp.float32),
            pltpu.VMEM((TAPS, templ * pitch, LANES), jnp.float32),
            pltpu.VMEM((local, 3 * LANES, WIDE), jnp.bfloat16),
            pltpu.VMEM((n, rows, OUT), jnp.float32),
            pltpu.VMEM((n, rows, OUT), jnp.float32),
            pltpu.SemaphoreType.DMA((4,)),
            pltpu.SemaphoreType.DMA,
            pltpu.SemaphoreType.DMA,
        ],
        compiler_params=pltpu.CompilerParams(collective_id=0, vmem_limit_bytes=16 << 20, has_side_effects=True),
    )(*[
        pltpu.with_memory_space_constraint(x, pltpu.HBM) for x in (records, templates, shifts, present)])


def solution(mesh):
    placed = (P("sta", None, "parts"), P(None, "sta", None, None), P(), P())
    return jax.shard_map(
        body, mesh=mesh, in_specs=placed, out_specs=P("sta", "parts"), check_vma=False
    )
```

```python
import functools
import math

import jax
import jax.numpy as jnp
from jax import lax
from jax.experimental import pallas as pl
from jax.experimental.pallas import tpu as pltpu
from jax.sharding import PartitionSpec as P

LEN = 600
WIN = 640
MAXSHIFT = 512
OUT = WIN - MAXSHIFT
LANES = 128
HALF = LANES // 2
TAPS = -(-LEN // LANES)
WIDE = WIN + TAPS * LANES


def window_sums(energy):
    powers = {1: energy}
    size = 1
    while size * 2 <= LEN:
        powers[size * 2] = powers[size] + pltpu.roll(powers[size], size, 1)
        size *= 2
    total, done = None, 0
    while size:
        if LEN & size:
            term = powers[size] if done == 0 else pltpu.roll(powers[size], done, 1)
            total = term if total is None else total + term
            done += size
        size //= 2
    return total


def mirrored(x):
    flip = LANES - 1 - lax.broadcasted_iota(jnp.int32, (x.shape[0], LANES), 1)
    tiles = [
        jnp.take_along_axis(x[:, i : i + LANES], flip, axis=1) for i in range(0, x.shape[1], LANES)
    ]
    return jnp.concatenate(tiles[::-1], axis=1)


def kernel(
    n, rec_hbm, tem_hbm, shift_hbm, present_hbm, out_ref,
    rec_in, tem_in, shift_v, present_s, rec, tem, hank, total, recv,
    in_sem, send_sem, recv_sem,
):
    me = lax.axis_index("sta")
    templ, local = tem_in.shape[0], tem_in.shape[2]
    rows = templ // n
    pitch = tem.shape[1] // templ
    samples = rec_in.shape[2]
    stations = n * local

    loads = [
        pltpu.make_async_copy(src, dst, in_sem.at[i])
        for i, (src, dst) in enumerate(
            [(rec_hbm, rec_in), (tem_hbm, tem_in), (shift_hbm, shift_v), (present_hbm, present_s)]
        )
    ]
    for load in loads:
        load.start()

    barrier = pltpu.get_barrier_semaphore()
    for step in range(1, n):
        pl.semaphore_signal(
            barrier, inc=1, device_id={"sta": lax.rem(me + step, n)},
            device_id_type=pl.DeviceIdType.MESH,
        )

    rec[...] = jnp.zeros_like(rec)
    tem[TAPS - 1] = jnp.zeros((templ * pitch, LANES), jnp.float32)

    loads[0].wait()
    for s in range(local):
        rec[s, 0:3, 0:samples] = rec_in[:, s].astype(jnp.float32)
    turned = [mirrored(rec[s]) for s in range(local)]
    energy = [jnp.sum(x * x, axis=0, keepdims=True) for x in turned]
    window = window_sums(jnp.concatenate(energy, axis=0))[:, WIDE - WIN :] / (3 * LEN)
    inv = lax.rsqrt(window + 1e-06)

    for s in range(local):
        for c in range(3):
            row = jnp.broadcast_to(turned[s][c : c + 1, :], (HALF, WIDE))
            slid = pltpu.roll(row, 0, 1, stride=1, stride_axis=0)
            hank[s, pl.ds(c * HALF, HALF), :] = slid.astype(jnp.bfloat16)

    loads[2].wait()
    loads[3].wait()
    lags_all = shift_v[...].astype(jnp.float32)
    column = lax.broadcasted_iota(jnp.int32, lags_all.shape, 1)
    lane = lax.broadcasted_iota(jnp.int32, (templ, LANES), 1)
    scale = math.sqrt(3 * LEN / stations) / (3 * LEN)
    places, flags = [], []
    for s in range(local):
        lag = jnp.sum(jnp.where(column == me * local + s, lags_all, 0.0), axis=1, keepdims=True)
        lag = jnp.broadcast_to(lag.astype(jnp.int32), (templ, LANES))
        places.append((lag // LANES, lane + lag % LANES))
        flags.append(present_s[me * local + s].astype(jnp.float32) * scale)

    loads[1].wait()
    for t in range(templ):
        for c in range(3):
            wave = tem_in[t, c].astype(jnp.float32)
            for a in range(TAPS):
                span = min(LANES, LEN - a * LANES)
                tem[a, pl.ds(pitch * t + local * c, local), 0:span] = wave[:, a * LANES : a * LANES + span]

    low = lane < HALF
    acc = jnp.zeros((templ, OUT), jnp.float32)
    for s in range(local):
        square = jnp.zeros((templ, LANES), jnp.float32)
        both = jnp.zeros((2 * templ, WIN + LANES), jnp.float32)
        for a in range(TAPS):
            pieces = [tem[a, pl.ds(local * c + s, templ, stride=pitch), :] for c in range(3)]
            square = square + sum(p * p for p in pieces)
            swapped = [pltpu.roll(p, HALF, 1) for p in pieces]
            upper = [jnp.where(low, pieces[0], swapped[1]), pieces[2]]
            lower = [jnp.where(low, swapped[0], pieces[1]), swapped[2]]
            left = jnp.concatenate(
                [jnp.concatenate(upper, axis=1), jnp.concatenate(lower, axis=1)], axis=0
            )[:, : 3 * HALF]
            both = both + jnp.dot(
                left.astype(jnp.bfloat16),
                hank[s, :, pl.ds(WIDE - WIN - (a + 1) * LANES, WIN + LANES)],
                preferred_element_type=jnp.float32,
            )
        raw = (both[:templ] + pltpu.roll(both[templ:], HALF, 1))[:, LANES:]
        power = jnp.sum(square, axis=1, keepdims=True) / (3 * LEN)
        ncc = raw * inv[s : s + 1, :]
        coarse, at = places[s]
        tiles = [ncc[:, i * LANES : (i + 1) * LANES] for i in range(WIN // LANES)][::-1]
        near, far = tiles[0], tiles[1]
        for i in range(1, len(tiles)):
            near = jnp.where(coarse == i, tiles[i], near)
            if i + 1 < len(tiles):
                far = jnp.where(coarse == i, tiles[i + 1], far)
        index = LANES - 1 - at % LANES
        picked = jnp.where(
            at < LANES,
            jnp.take_along_axis(near, index, axis=1),
            jnp.take_along_axis(far, index, axis=1),
        )
        acc = acc + picked * (lax.rsqrt(power + 1e-06) * flags[s])
    for d in range(n):
        total[d] = acc[d * rows : (d + 1) * rows]

    pl.semaphore_wait(barrier, n - 1)
    for step in range(1, n):
        to = lax.rem(me + step, n)
        pltpu.make_async_remote_copy(
            src_ref=total.at[to], dst_ref=recv.at[step], send_sem=send_sem, recv_sem=recv_sem,
            device_id={"sta": to}, device_id_type=pl.DeviceIdType.MESH,
        ).start()
    rest = recv.at[pl.ds(1, n - 1)]
    pltpu.make_async_copy(rest, rest, recv_sem).wait()
    pltpu.make_async_copy(rest, rest, send_sem).wait()
    out_ref[...] = total[me] + jnp.sum(recv[pl.ds(1, n - 1)], axis=0)


def body(records, templates, shifts, present):
    n = lax.axis_size("sta")
    templ, local = templates.shape[0], templates.shape[1]
    rows = templ // n
    pitch = -(-3 * local // 8) * 8
    records = records.transpose(1, 0, 2)
    templates = templates.transpose(0, 2, 1, 3)
    hbm = pl.BlockSpec(memory_space=pl.ANY)
    return pl.pallas_call(
        functools.partial(kernel, n),
        out_shape=jax.ShapeDtypeStruct((rows, OUT), jnp.float32),
        in_specs=[hbm] * 4,
        out_specs=pl.BlockSpec(memory_space=pltpu.VMEM),
        scratch_shapes=[
            pltpu.VMEM(records.shape, records.dtype),
            pltpu.VMEM(templates.shape, templates.dtype),
            pltpu.VMEM(shifts.shape, shifts.dtype),
            pltpu.SMEM(present.shape, present.dtype),
            pltpu.VMEM((local, 8, WIDE), jnp.float32),
            pltpu.VMEM((TAPS, templ * pitch, LANES), jnp.float32),
            pltpu.VMEM((local, 3 * HALF, WIDE), jnp.bfloat16),
            pltpu.VMEM((n, rows, OUT), jnp.float32),
            pltpu.VMEM((n, rows, OUT), jnp.float32),
            pltpu.SemaphoreType.DMA((4,)),
            pltpu.SemaphoreType.DMA,
            pltpu.SemaphoreType.DMA,
        ],
        compiler_params=pltpu.CompilerParams(collective_id=0, vmem_limit_bytes=16 << 20, has_side_effects=True),
    )(*[
        pltpu.with_memory_space_constraint(x, pltpu.HBM) for x in (records, templates, shifts, present)])


def solution(mesh):
    placed = (P("sta", None, "parts"), P(None, "sta", None, None), P(), P())
    return jax.shard_map(
        body, mesh=mesh, in_specs=placed, out_specs=P("sta", "parts"), check_vma=False
    )
```
